128 devices in a mesh: seq: 64 (over x_lo, z, y, core), head: 2 (over x_hi).
Axes of the slice: x: 4 (x_hi: 2, x_lo: 2; x = x_hi * 2 + x_lo), y: 4, z: 4, core: 2. Of those that a mesh axis runs over, the one named last changes fastest.
Arguments:
- query_tensor: float32 [32768, 32, 128], P('seq', 'head'), may hold values from -6 to 6
- key_tensor: float32 [32768, 16, 128], P('seq', 'head'), may hold values from -6 to 6
- value_tensor: float32 [32768, 16, 128], P('seq', 'head'), may hold values from -6 to 6
- output_gradient: float32 [32768, 32, 128], P('seq', 'head'), may hold values from -24 to 24
- logsumexp: float32 [32, 32768], P('head', 'seq'), may hold values from 5.5 to 7
- row_inner_products: float32 [32, 32768], P('head', 'seq'), may hold values from -120 to 120
Outputs:
- query_grad: float32 [32768, 32, 128], P('seq', 'head')
- key_grad: float32 [32768, 16, 128], P('seq', 'head')
- value_grad: float32 [32768, 16, 128], P('seq', 'head')
The draws below stay inside these ranges and needn't reach their ends.
All inputs are finite; a program needn't handle non-finite values.
Results may differ from the reference program's by a relative error of at most 0.0053.
Values may be sent and summed in bfloat16 or wider, within the bound.
No kernel may reach another device: no remote copies, remote signals or barrier semaphores. Data moves between devices by JAX's collectives and lax.ppermute only.
A program may use at most 192 MiB of HBM per device.

```python
import jax
import jax.numpy as jnp
from jax import lax

QUERY_HEADS = 32
KEY_VALUE_HEADS = 16
HEAD_SIZE = 128
WINDOW = 1024
QSCALE = 168
TOK_DEV = 512
SEQUENCE_TOKENS = 32768


def block_scale(own_key, dims, pieces, low, high):
    def one(dim, shards_of):
        steps = jax.random.uniform(jax.random.fold_in(jax.random.fold_in(own_key, 6), dim), (shards_of,), jnp.float32, low / len(pieces), high / len(pieces))
        return jnp.repeat(jnp.exp(steps), dims[dim] // shards_of).reshape((-1,) + (1,) * (len(dims) - dim - 1))

    loudness = one(*pieces[0])
    for cut in pieces[1:]:
        loudness = loudness * one(*cut)
    return loudness


def normal_values(rng, extent, scale, most, pieces=(), held_as=jnp.bfloat16):
    gain = block_scale(rng, extent, pieces, -0.22, 0.18) if pieces else 1.0
    array = jax.random.normal(rng, extent, jnp.float32) * scale * gain
    return jnp.minimum(jnp.maximum(array, -most), most).astype(held_as)


def setup_inputs(seed: int = 0) -> dict:
    splits = jax.random.split(jax.random.key(seed), 7)
    query_tensor = normal_values(splits[0], (SEQUENCE_TOKENS, QUERY_HEADS, HEAD_SIZE), 1.0, 6.0, ((0, 64), (1, 2)), jnp.float32)
    key_tensor = normal_values(splits[1], (SEQUENCE_TOKENS, KEY_VALUE_HEADS, HEAD_SIZE), 1.0, 6.0, ((0, 64), (1, 2)), jnp.float32)
    value_tensor = normal_values(splits[2], (SEQUENCE_TOKENS, KEY_VALUE_HEADS, HEAD_SIZE), 1.0, 6.0, ((0, 64), (1, 2)), jnp.float32)
    output_gradient = normal_values(splits[3], (SEQUENCE_TOKENS, QUERY_HEADS, HEAD_SIZE), 4.0, 24.0, ((0, 64), (1, 2)), jnp.float32)
    logsumexp = jnp.clip(5.5 + 1.5 * jax.random.uniform(splits[4], (QUERY_HEADS, SEQUENCE_TOKENS), jnp.float32) ** block_scale(splits[4], (QUERY_HEADS, SEQUENCE_TOKENS), ((0, 2), (1, 64)), -0.2, 0.2), 5.5, 7.0)
    row_inner_products = normal_values(splits[5], (QUERY_HEADS, SEQUENCE_TOKENS), 20.0, 120.0, ((0, 2), (1, 64)), jnp.float32)
    return dict(query_tensor=query_tensor, key_tensor=key_tensor, value_tensor=value_tensor, output_gradient=output_gradient, logsumexp=logsumexp, row_inner_products=row_inner_products)


def block_terms(query_rows, gradient_list, lse_rows, output_dots, keys, values, allowed):
    scale = QSCALE ** -0.5
    scores = jnp.einsum('tkgd,skd->kgts', query_rows.astype(jnp.float32), keys.astype(jnp.float32))
    probs = jnp.where(allowed, jnp.exp(scale * scores - lse_rows[..., None]), 0.0)
    dprob = jnp.einsum('tkgd,skd->kgts', gradient_list.astype(jnp.float32), values.astype(jnp.float32))
    dscore = probs * (dprob - output_dots[..., None])
    probs_low = probs.astype(jnp.bfloat16).astype(jnp.float32)
    dscore_low = dscore.astype(jnp.bfloat16).astype(jnp.float32)
    dvalue = jnp.einsum('kgts,tkgd->skd', probs_low, gradient_list.astype(jnp.float32))
    dkey = scale * jnp.einsum('kgts,tkgd->skd', dscore_low, query_rows.astype(jnp.float32))
    dquery = scale * jnp.einsum('kgts,skd->tkgd', dscore_low, keys.astype(jnp.float32))
    return dquery, dkey, dvalue


def reference(query_tensor, key_tensor, value_tensor, output_gradient, logsumexp, row_inner_products):
    window_length = TOK_DEV
    blocks = SEQUENCE_TOKENS // window_length
    query_group = QUERY_HEADS // KEY_VALUE_HEADS
    query_rows = query_tensor.astype(jnp.bfloat16).reshape(SEQUENCE_TOKENS, KEY_VALUE_HEADS, query_group, HEAD_SIZE)
    gradient_list = output_gradient.astype(jnp.bfloat16).reshape(SEQUENCE_TOKENS, KEY_VALUE_HEADS, query_group, HEAD_SIZE)
    front_edge = jnp.zeros((2 * window_length, KEY_VALUE_HEADS, HEAD_SIZE), jnp.bfloat16)
    keys = jnp.concatenate([front_edge, key_tensor.astype(jnp.bfloat16)], 0)
    values = jnp.concatenate([front_edge, value_tensor.astype(jnp.bfloat16)], 0)
    log_sum_exponent = logsumexp.reshape(KEY_VALUE_HEADS, query_group, SEQUENCE_TOKENS)
    output_dots = row_inner_products.reshape(KEY_VALUE_HEADS, query_group, SEQUENCE_TOKENS)

    def advance(carry, index):
        dkey_all, dvalue_all = carry
        start = (index * window_length).astype(jnp.int32)
        query_block = lax.dynamic_slice_in_dim(query_rows, start, window_length, 0)
        grad_block = lax.dynamic_slice_in_dim(gradient_list, start, window_length, 0)
        lse_block = lax.dynamic_slice_in_dim(log_sum_exponent, start, window_length, 2)
        dots_block = lax.dynamic_slice_in_dim(output_dots, start, window_length, 2)
        key_block = lax.dynamic_slice_in_dim(keys, start, 3 * window_length, 0)
        value_block = lax.dynamic_slice_in_dim(values, start, 3 * window_length, 0)
        qpos = start + lax.broadcasted_iota(jnp.int32, (window_length, 3 * window_length), 0)
        kpos = start - 2 * window_length + lax.broadcasted_iota(jnp.int32, (window_length, 3 * window_length), 1)
        spread = qpos - kpos
        allowed = (spread >= 0) & (spread < WINDOW) & (kpos >= 0)
        dquery, dkey, dvalue = block_terms(query_block, grad_block, lse_block, dots_block, key_block, value_block, allowed)
        dkey_all = lax.dynamic_update_slice_in_dim(dkey_all, lax.dynamic_slice_in_dim(dkey_all, start, 3 * window_length, 0) + dkey, start, 0)
        dvalue_all = lax.dynamic_update_slice_in_dim(dvalue_all, lax.dynamic_slice_in_dim(dvalue_all, start, 3 * window_length, 0) + dvalue, start, 0)
        return (dkey_all, dvalue_all), dquery

    empty_buffer = jnp.zeros((SEQUENCE_TOKENS + 2 * window_length, KEY_VALUE_HEADS, HEAD_SIZE), jnp.float32)
    (dkey_all, dvalue_all), dqueries = lax.scan(advance, (empty_buffer, empty_buffer), jnp.arange(blocks, dtype=jnp.int32))
    return dqueries.reshape(SEQUENCE_TOKENS, QUERY_HEADS, HEAD_SIZE), dkey_all[2 * window_length:], dvalue_all[2 * window_length:]
```

```python
import math

import jax
import jax.numpy as jnp
from jax import lax
from jax.experimental import pallas as pl
from jax.experimental.pallas import tpu as pltpu
from jax.sharding import PartitionSpec as P

WINDOW = 1024
QSCALE = 168
SCALE = QSCALE ** (-0.5)
LOG2E = math.log2(math.e)
TILE = 256
CHUNKS = (2, 2, 2, 2)
F32, BF16 = jnp.float32, jnp.bfloat16
NT = (((1,), (1,)), ((), ()))
NN = (((1,), (0,)), ((), ()))


def dot(a, b, dims):
    return lax.dot_general(a, b, dims, preferred_element_type=F32)


def rotated(x, by):
    count = lax.axis_size("seq")
    return lax.ppermute(x, "seq", [(i, (i + by) % count) for i in range(count)])


def partner(x):
    count = lax.axis_size("seq")
    return lax.ppermute(x, "seq", [(i, i ^ 1) for i in range(count)])


def head_major(first, second, sizes, whole):
    tokens, heads, width = first.shape
    views = [x.reshape(tokens, heads, 1, width) for x in (first, second)]

    def body(a, b, *rest):
        outs = rest[: len(sizes) + whole]
        wide, narrow, in_sem, out_sem, part_sem = rest[len(sizes) + whole :]

        def load(h, t):
            return pltpu.make_async_copy((a, b)[t].at[:, h, 0, :], wide.at[h, t], in_sem.at[h, t])

        for h in range(heads):
            for t in range(2):
                load(h, t).start()
        waits = []
        where = [(c, i) for c, n in enumerate(sizes) for i in range(n)]
        for h in range(heads):
            for t in range(2):
                load(h, t).wait()
                narrow[h, t] = wide[h, t].astype(BF16)
            if sizes:
                c, i = where[h]
                waits.append(pltpu.make_async_copy(narrow.at[h], outs[c].at[i], part_sem.at[h]))
                waits[-1].start()
            if whole:
                waits.append(pltpu.make_async_copy(narrow.at[h], outs[-1].at[h], out_sem.at[h]))
                waits[-1].start()
        for w in waits:
            w.wait()

    shapes = [jax.ShapeDtypeStruct((n, 2, tokens, width), BF16) for n in sizes]
    if whole:
        shapes.append(jax.ShapeDtypeStruct((heads, 2, tokens, width), BF16))
    return pl.pallas_call(
        body,
        out_shape=shapes,
        in_specs=[pl.BlockSpec(memory_space=pl.ANY)] * 2,
        out_specs=[pl.BlockSpec(memory_space=pl.ANY)] * len(shapes),
        scratch_shapes=[
            pltpu.VMEM((heads, 2, tokens, width), F32),
            pltpu.VMEM((heads, 2, tokens, width), BF16),
            pltpu.SemaphoreType.DMA((heads, 2)),
            pltpu.SemaphoreType.DMA((heads,)),
            pltpu.SemaphoreType.DMA((heads,)),
        ],
        cost_estimate=pl.CostEstimate(flops=0, transcendentals=0, bytes_accessed=tokens * heads * width * 12),
        name="head_major",
    )(*views)


def attend(at, size, place, qg, lse, dots, own, swapped_own, swapped_far, far, query_grad):
    tokens, width = far.shape[2], far.shape[3]
    half = tokens // 2

    def body(place_ref, qg_ref, lse_ref, dots_ref, own_ref, so_ref, sf_ref, far_ref, *rest):
        dq_hbm, gown, gnear, gfar, dq_buf, sem = rest[-6:]
        h = pl.program_id(0)
        slot = lax.rem(h, 2)

        def flush(s, hh, j):
            return pltpu.make_async_copy(dq_buf.at[s, j], dq_hbm.at[:, 2 * (at + hh) + j, 0, :], sem.at[s, j])

        @pl.when(h >= 2)
        def _():
            for j in range(2):
                flush(slot, h - 2, j).wait()

        pos = place_ref[0]
        even = lax.rem(pos, 2) == 0
        away = {
            "o": 0.0,
            "n": jnp.where(pos >= 1, 0.0, 1e30).astype(F32),
            "f": jnp.where(pos >= 2, 0.0, 1e30).astype(F32),
        }
        rows = lax.broadcasted_iota(jnp.int32, (half, half), 0)
        cols = lax.broadcasted_iota(jnp.int32, (half, half), 1)
        later = rows > cols
        grads = {"o": gown, "n": gnear, "f": gfar}
        kb, vb = {}, {}
        for i in range(2):
            sl = slice(i * half, (i + 1) * half)
            kb["o", i], vb["o", i] = own_ref[0, sl, :], own_ref[1, sl, :]
            kb["f", i], vb["f", i] = far_ref[0, sl, :], far_ref[1, sl, :]
            kb["n", i] = jnp.where(even, sf_ref[0, sl, :], so_ref[0, sl, :])
            vb["n", i] = jnp.where(even, sf_ref[1, sl, :], so_ref[1, sl, :])
        kt = {x: kb[x].T for x in kb}
        dk, dv = {x: [] for x in kb}, {x: [] for x in kb}
        for j in range(2):
            l2 = lse_ref[j : j + 1, :] * LOG2E
            dd = dots_ref[j : j + 1, :]
            for i in range(2):
                sl = slice(i * half, (i + 1) * half)
                q, g = qg_ref[j, 0, sl, :], qg_ref[j, 1, sl, :]
                pairs = [("f", 0)] * (i == 0) + [("f", 1), ("n", 0), ("n", 1), ("o", 0)] + [("o", 1)] * (i == 1)
                terms = []
                for x in pairs:
                    l = l2[:, sl] + away[x[0]] if x[0] != "o" else l2[:, sl]
                    st = dot(kb[x], q, NT)
                    dpt = dot(vb[x], g, NT)
                    p = jnp.exp2(st * (SCALE * LOG2E) - l)
                    if x == ("f", i):
                        p = jnp.where(later, p, 0.0)
                    elif x == ("o", i):
                        p = jnp.where(later, 0.0, p)
                    ds = (p * (dpt - dd[:, sl])).astype(BF16)
                    dv[x].append((p.astype(BF16), g))
                    dk[x].append((ds, q))
                    terms.append((kt[x], ds))
                dqt = sum(dot(a, b, NN) for a, b in terms)
                dq_buf[slot, j, sl, :] = (dqt * SCALE).T
        for x in kb:
            sl = slice(x[1] * half, (x[1] + 1) * half)
            out = grads[x[0]]
            out[0, sl, :] = (sum(dot(a, b, NN) for a, b in dk[x]) * SCALE).astype(out.dtype)
            out[1, sl, :] = sum(dot(a, b, NN) for a, b in dv[x]).astype(out.dtype)
        for j in range(2):
            flush(slot, h, j).start()

        @pl.when(h == size - 1)
        def _():
            for j in range(2):
                if size > 1:
                    flush(1 - slot, h - 1, j).wait()
                flush(slot, h, j).wait()

    here = pl.BlockSpec((None, 2, tokens, width), lambda h: (h, 0, 0, 0))
    there = pl.BlockSpec((None, 2, tokens, width), lambda h: (h + at, 0, 0, 0))
    rows = pl.BlockSpec((None, 2, tokens), lambda h: (h + at, 0, 0))
    hbm = pl.BlockSpec(memory_space=pl.ANY)
    operands = [place, qg, lse, dots, own, swapped_own, swapped_far, far]
    in_specs = [
        pl.BlockSpec(memory_space=pltpu.SMEM),
        pl.BlockSpec((2, 2, tokens, width), lambda h: (h + at, 0, 0, 0)),
        rows,
        rows,
        there,
        there,
        here,
        here,
    ]
    aliases = {}
    if query_grad is not None:
        operands.append(query_grad)
        in_specs.append(hbm)
        aliases = {8: 0}
    return pl.pallas_call(
        body,
        grid=(size,),
        in_specs=in_specs,
        out_specs=[hbm, here, here, here],
        out_shape=[
            jax.ShapeDtypeStruct((tokens, qg.shape[0], 1, width), F32),
            jax.ShapeDtypeStruct((size, 2, tokens, width), F32),
            jax.ShapeDtypeStruct((size, 2, tokens, width), BF16),
            jax.ShapeDtypeStruct((size, 2, tokens, width), BF16),
        ],
        scratch_shapes=[pltpu.VMEM((2, 2, tokens, width), F32), pltpu.SemaphoreType.DMA((2, 2))],
        input_output_aliases=aliases,
        cost_estimate=pl.CostEstimate(
            flops=size * 2 * 10 * 5 * 2 * half * half * width,
            transcendentals=size * 2 * 10 * half * half,
            bytes_accessed=size * tokens * width * 40,
        ),
        name="attend",
    )(*operands)


def settle(at, size, place, own, near, back, key_grad, value_grad, heads):
    tokens, width = own.shape[2], own.shape[3]

    def body(place_ref, own_ref, near_ref, back_ref, *rest):
        outs, buf, sem = rest[-4:-2], rest[-2], rest[-1]
        even = lax.rem(place_ref[0], 2) == 0
        copies = []
        for h in range(size):
            for t in range(2):
                near_term = jnp.where(even, near_ref[h, t].astype(F32), 0.0)
                buf[h, t] = own_ref[h, t] + near_term + back_ref[h, t].astype(F32)
                copies.append(pltpu.make_async_copy(buf.at[h, t], outs[t].at[:, at + h, 0, :], sem.at[h, t]))
                copies[-1].start()
        for c in copies:
            c.wait()

    hbm = pl.BlockSpec(memory_space=pl.ANY)
    vmem = pl.BlockSpec(memory_space=pltpu.VMEM)
    operands = [place, own, near, back]
    in_specs = [pl.BlockSpec(memory_space=pltpu.SMEM), vmem, vmem, vmem]
    aliases = {}
    if key_grad is not None:
        operands += [key_grad, value_grad]
        in_specs += [hbm, hbm]
        aliases = {4: 0, 5: 1}
    return pl.pallas_call(
        body,
        in_specs=in_specs,
        out_specs=[hbm, hbm],
        out_shape=[jax.ShapeDtypeStruct((tokens, heads, 1, width), F32)] * 2,
        scratch_shapes=[pltpu.VMEM((size, 2, tokens, width), F32), pltpu.SemaphoreType.DMA((size, 2))],
        input_output_aliases=aliases,
        cost_estimate=pl.CostEstimate(flops=0, transcendentals=0, bytes_accessed=size * tokens * width * 24),
        name="settle",
    )(*operands)


def on_device(query_tensor, key_tensor, value_tensor, output_gradient, logsumexp, row_inner_products):
    tokens, qheads, width = query_tensor.shape
    kheads = key_tensor.shape[1]
    position = lax.axis_index("seq")
    place = position.astype(jnp.int32).reshape(1)
    odd = position % 2 == 1
    *parts, own = head_major(key_tensor, value_tensor, CHUNKS, True)
    far = [rotated(x, 2) for x in parts]
    swapped_own = partner(own)
    (qg,) = head_major(query_tensor, output_gradient, (), True)
    lse = logsumexp.reshape(kheads, 2, tokens)
    dots = row_inner_products.reshape(kheads, 2, tokens)
    query_grad = key_grad = value_grad = None
    at = 0
    for c, size in enumerate(CHUNKS):
        swapped_far = partner(far[c])
        query_grad, gown, gnear, gfar = attend(
            at, size, place, qg, lse, dots, own, swapped_own, swapped_far, far[c], query_grad
        )
        near = partner(gnear)
        owed = jnp.where(odd, gfar.astype(F32) + near.astype(F32), gfar.astype(F32)).astype(BF16)
        back = rotated(owed, -2)
        key_grad, value_grad = settle(at, size, place, gown, near, back, key_grad, value_grad, kheads)
        at += size
    return (
        query_grad.reshape(tokens, qheads, width),
        key_grad.reshape(tokens, kheads, width),
        value_grad.reshape(tokens, kheads, width),
    )


def solution(mesh):
    return jax.shard_map(
        on_device,
        mesh=mesh,
        in_specs=(
            P("seq", "head", None),
            P("seq", "head", None),
            P("seq", "head", None),
            P("seq", "head", None),
            P("head", "seq"),
            P("head", "seq"),
        ),
        out_specs=(P("seq", "head", None), P("seq", "head", None), P("seq", "head", None)),
        check_vma=False,
    )
```

```python
import math

import jax
import jax.numpy as jnp
from jax import lax
from jax.experimental import pallas as pl
from jax.experimental.pallas import tpu as pltpu
from jax.sharding import PartitionSpec as P


QSCALE = 168
SCALE = QSCALE ** (-0.5)
LOG2E = math.log2(math.e)
VMEM = 64 * 1000 * 1024
GROUPS = (1, 1, 2)
MINE = 4
F32, BF16 = jnp.float32, jnp.bfloat16
NT = (((1,), (1,)), ((), ()))
NN = (((1,), (0,)), ((), ()))
HBM = pl.BlockSpec(memory_space=pl.ANY)
SCALAR = pl.BlockSpec(memory_space=pltpu.SMEM)
PARAMS = pltpu.CompilerParams(vmem_limit_bytes=VMEM)


def dot(a, b, dims):
    return lax.dot_general(a, b, dims, preferred_element_type=F32)


def rotated(x, by):
    count = lax.axis_size("seq")
    return lax.ppermute(x, "seq", [(i, (i + by) % count) for i in range(count)])


def crossed(x, by):
    count = lax.axis_size("seq")
    return lax.ppermute(x, "seq", [(i, ((i + by) % count) ^ 1) for i in range(count)])


def partner(x):
    count = lax.axis_size("seq")
    return lax.ppermute(x, "seq", [(i, i ^ 1) for i in range(count)])


def cost(nbytes, flops=0, exps=0):
    return pl.CostEstimate(flops=flops, transcendentals=exps, bytes_accessed=nbytes)


def like(shape, dtype):
    return jax.ShapeDtypeStruct(shape, dtype)


def pack_kv(place, keys, values, lse, dots):
    tokens, heads, _, width = keys.shape

    def body(place_ref, k, v, lse_ref, dots_ref, *rest):
        keep, *parts, give, rows = rest[: 3 + 2 * len(GROUPS)]
        wide, narrow, rows_buf, in_sem, out_sem, part_sem, row_sem = rest[3 + 2 * len(GROUPS) :]
        spots = [(c, x) for c, n in enumerate(GROUPS) for x in range(n)]
        core = lax.rem(place_ref[0], 2)
        order = [(part, i) for part in range(2) for i in range(MINE)]

        def load(n, t):
            part, i = order[n]
            half = 1 - core if part == 0 else core
            return pltpu.make_async_copy((k, v)[t].at[:, half * MINE + i, 0, :], wide.at[n, t], in_sem.at[n, t])

        for n in range(len(order)):
            for t in range(2):
                load(n, t).start()
        rows_buf[0] = lse_ref[...]
        rows_buf[1] = dots_ref[...]
        waits = [pltpu.make_async_copy(rows_buf, rows, row_sem)]
        waits[0].start()
        for n, (part, i) in enumerate(order):
            for t in range(2):
                load(n, t).wait()
                narrow[n, t] = wide[n, t].astype(BF16)
            c, x = spots[i]
            target = parts[c if part else len(GROUPS) + c].at[x]
            waits.append(pltpu.make_async_copy(narrow.at[n], target, part_sem.at[n]))
            waits[-1].start()
            waits.append(pltpu.make_async_copy(narrow.at[n], (give, keep)[part].at[i], out_sem.at[n]))
            waits[-1].start()
        for w in waits:
            w.wait()

    return pl.pallas_call(
        body,
        in_specs=[SCALAR, HBM, HBM, pl.BlockSpec(memory_space=pltpu.VMEM), pl.BlockSpec(memory_space=pltpu.VMEM)],
        out_specs=[HBM] * (3 + 2 * len(GROUPS)),
        out_shape=[
            like((MINE, 2, tokens, width), BF16),
            *[like((n, 2, tokens, width), BF16) for n in GROUPS] * 2,
            like((MINE, 2, tokens, width), BF16),
            like((2, *lse.shape), F32),
        ],
        scratch_shapes=[
            pltpu.VMEM((2 * MINE, 2, tokens, width), F32),
            pltpu.VMEM((2 * MINE, 2, tokens, width), BF16),
            pltpu.VMEM((2, *lse.shape), F32),
            pltpu.SemaphoreType.DMA((2 * MINE, 2)),
            pltpu.SemaphoreType.DMA((2 * MINE,)),
            pltpu.SemaphoreType.DMA((2 * MINE,)),
            pltpu.SemaphoreType.DMA,
        ],
        compiler_params=PARAMS,
        cost_estimate=cost(tokens * heads * width * 12),
        name="pack_kv",
    )(place, keys, values, lse, dots)


def pack_qg(give, place, queries, gradients):
    tokens, _, _, width = queries.shape

    def body(place_ref, q, g, out, wide, narrow, in_sem, out_sem):
        core = lax.rem(place_ref[0], 2)
        half = 1 - core if give else core
        order = [(i, j, t) for i in range(MINE) for j in range(2) for t in range(2)]

        def load(i, j, t):
            return pltpu.make_async_copy(
                (q, g)[t].at[:, 2 * (half * MINE + i) + j, 0, :], wide.at[i, j, t], in_sem.at[i, j, t]
            )

        for o in order:
            load(*o).start()
        waits = []
        for i in range(MINE):
            for j in range(2):
                for t in range(2):
                    load(i, j, t).wait()
                    narrow[i, j, t] = wide[i, j, t].astype(BF16)
            waits.append(pltpu.make_async_copy(narrow.at[i], out.at[i], out_sem.at[i]))
            waits[-1].start()
        for w in waits:
            w.wait()

    shape = (MINE, 2, 2, tokens, width)
    return pl.pallas_call(
        body,
        in_specs=[SCALAR, HBM, HBM],
        out_specs=HBM,
        out_shape=like(shape, BF16),
        scratch_shapes=[
            pltpu.VMEM(shape, F32),
            pltpu.VMEM(shape, BF16),
            pltpu.SemaphoreType.DMA(shape[:3]),
            pltpu.SemaphoreType.DMA((MINE,)),
        ],
        compiler_params=PARAMS,
        cost_estimate=cost(math.prod(shape) * 6),
        name="pack_qg",
    )(place, queries, gradients)


def attend(i, slot, place, qg_mine, qg_theirs, rows_mine, rows_theirs, kv_mine, kv_theirs, far_mine, far_theirs, query_grad, sent_dq):
    tokens, width = kv_mine.shape[2:]
    half = tokens // 2
    first = query_grad is None

    def body(place_ref, qm, qt, rm, rt, km, kt_, fm, ft, *rest):
        own, far, dq_out, dq_sent = rest[-16:-12]
        qg, rows_buf, keys, buf, low, own_buf, far_buf, in_sem, sem, low_sem, own_sem, far_sem = rest[-12:]
        pos = place_ref[0]
        core = lax.rem(pos, 2)
        gate = jnp.where(pos >= 2, 0.0, 1e30).astype(F32)
        head = core * MINE + i
        sides = ((core, 0), (1 - core, 1))
        copy = pltpu.make_async_copy
        loads = [copy((rm, rt)[x], rows_buf.at[n], in_sem.at[x]) for n, x in sides]
        loads += [copy((km, kt_)[x].at[i], keys.at[0, n], in_sem.at[2 + x]) for n, x in sides]
        loads += [copy((fm, ft)[x].at[slot], keys.at[1, n], in_sem.at[4 + x]) for n, x in sides]
        q_loads = [[copy((qm, qt)[x].at[i, j], qg.at[j, n], in_sem.at[6 + 2 * j + x]) for n, x in sides] for j in range(2)]
        for c in loads + q_loads[0] + q_loads[1]:
            c.start()
        for c in loads:
            c.wait()
        rows = lax.broadcasted_iota(jnp.int32, (half, half), 0)
        cols = lax.broadcasted_iota(jnp.int32, (half, half), 1)
        later = rows > cols
        cut = [(a // 2, slice((a % 2) * half, (a % 2 + 1) * half)) for a in range(4)]
        tiles = [(e, a) for e in range(2) for a in range(4)]
        kb = {(e, a): keys[e, cut[a][0], 0, cut[a][1], :] for e, a in tiles}
        vb = {(e, a): keys[e, cut[a][0], 1, cut[a][1], :] for e, a in tiles}
        kt = {x: kb[x].T for x in tiles}
        dk, dv = {x: [] for x in tiles}, {x: [] for x in tiles}
        out_copies = []
        for j in range(2):
            for c in q_loads[j]:
                c.wait()
            row = pl.ds(2 * head + j, 1)
            for b, (n, sl) in enumerate(cut):
                q, g = qg[j, n, 0, sl, :], qg[j, n, 1, sl, :]
                l = rows_buf[n, 0, row, sl] * LOG2E
                d = rows_buf[n, 1, row, sl]
                dqt = []
                for e, a in [(0, a) for a in range(b + 1)] + [(1, a) for a in range(b, 4)]:
                    p = jnp.exp2(dot(kb[e, a], q, NT) * (SCALE * LOG2E) - (l + gate if e else l))
                    if a == b:
                        p = jnp.where(later, p, 0.0) if e else jnp.where(later, 0.0, p)
                    ds = (p * (dot(vb[e, a], g, NT) - d)).astype(BF16)
                    dv[e, a].append((p.astype(BF16), g))
                    dk[e, a].append((ds, q))
                    dqt.append((kt[e, a], ds))
                x = (sum(dot(x, y, NN) for x, y in dqt) * SCALE).T
                buf[n, j, sl, :] = x
                low[n, j, sl, :] = x.astype(BF16)
            out_copies.append(copy(buf.at[core, j], dq_out.at[:, 2 * head + j, 0, :], sem.at[j]))
            out_copies.append(copy(low.at[1 - core, j], dq_sent.at[i, j], low_sem.at[j]))
            for c in out_copies[-2:]:
                c.start()
        for e in (1, 0):
            for t in range(2):
                for a in range(4):
                    x = sum(dot(x, y, NN) for x, y in (dv if t else dk)[e, a])
                    where = slice(a * half, (a + 1) * half)
                    if e:
                        far_buf[t, where, :] = (x if t else x * SCALE).astype(BF16)
                    else:
                        own_buf[t, where, :] = x if t else x * SCALE
                out_copies.append(copy((own_buf, far_buf)[e].at[t], (own, far)[e].at[t], (own_sem, far_sem)[e].at[t]))
                out_copies[-1].start()
        for c in out_copies:
            c.wait()

    operands = [place, qg_mine, qg_theirs, rows_mine, rows_theirs, kv_mine, kv_theirs, far_mine, far_theirs]
    in_specs = [SCALAR] + [HBM] * 8
    if not first:
        operands += [query_grad, sent_dq]
        in_specs += [HBM, HBM]
    return pl.pallas_call(
        body,
        in_specs=in_specs,
        out_specs=[HBM] * 4,
        out_shape=[
            like((2, 2 * tokens, width), F32),
            like((2, 2 * tokens, width), BF16),
            like((tokens, 4 * MINE, 1, width), F32),
            like((MINE, 2, tokens, width), BF16),
        ],
        scratch_shapes=[
            pltpu.VMEM((2, 2, 2, tokens, width), BF16),
            pltpu.VMEM((2, *rows_mine.shape), F32),
            pltpu.VMEM((2, 2, 2, tokens, width), BF16),
            pltpu.VMEM((2, 2, tokens, width), F32),
            pltpu.VMEM((2, 2, tokens, width), BF16),
            pltpu.VMEM((2, 2 * tokens, width), F32),
            pltpu.VMEM((2, 2 * tokens, width), BF16),
            pltpu.SemaphoreType.DMA((10,)),
            pltpu.SemaphoreType.DMA((2,)),
            pltpu.SemaphoreType.DMA((2,)),
            pltpu.SemaphoreType.DMA((2,)),
            pltpu.SemaphoreType.DMA((2,)),
        ],
        input_output_aliases={} if first else {9: 2, 10: 3},
        compiler_params=PARAMS,
        cost_estimate=cost(tokens * width * 40, 2 * 20 * 5 * 2 * half**2 * width, 2 * 20 * half**2),
        name="attend",
    )(*operands)


def finish(heads, place, owns, backs, key_grad, value_grad):
    tokens, width = owns[0].shape[1] // 2, owns[0].shape[2]
    n = len(heads)
    first = key_grad is None

    def body(place_ref, *rest):
        own_refs, back_refs, (dk, dv, send) = rest[:n], rest[n : 2 * n], rest[-10:-7]
        own_buf, back_buf, out_buf, low, in_sem, out_sem, low_sem = rest[-7:]
        core = lax.rem(place_ref[0], 2)
        order = [(x, side, t) for x in range(n) for side in range(2) for t in range(2)]

        def loads(x, side, t):
            where = pl.ds(pl.multiple_of((core if side else 1 - core) * tokens, tokens), tokens)
            return [
                pltpu.make_async_copy(own_refs[x].at[t, where, :], own_buf.at[x, side, t], in_sem.at[0, x, side, t]),
                pltpu.make_async_copy(back_refs[x].at[t, where, :], back_buf.at[x, side, t], in_sem.at[1, x, side, t]),
            ]

        for o in order:
            for c in loads(*o):
                c.start()
        waits = []
        for x, side, t in order:
            for c in loads(x, side, t):
                c.wait()
            total = own_buf[x, side, t] + back_buf[x, side, t].astype(F32)
            if side:
                out_buf[x, t] = total
                target = (dk, dv)[t].at[:, core * MINE + heads[x], 0, :]
                waits.append(pltpu.make_async_copy(out_buf.at[x, t], target, out_sem.at[x, t]))
            else:
                low[x, t] = total.astype(BF16)
                waits.append(pltpu.make_async_copy(low.at[x, t], send.at[x, t], low_sem.at[x, t]))
            waits[-1].start()
        for w in waits:
            w.wait()

    operands = [place, *owns, *backs]
    in_specs = [SCALAR] + [HBM] * (2 * n)
    if not first:
        operands += [key_grad, value_grad]
        in_specs += [HBM, HBM]
    return pl.pallas_call(
        body,
        in_specs=in_specs,
        out_specs=[HBM] * 3,
        out_shape=[like((tokens, 2 * MINE, 1, width), F32)] * 2 + [like((n, 2, tokens, width), BF16)],
        scratch_shapes=[
            pltpu.VMEM((n, 2, 2, tokens, width), F32),
            pltpu.VMEM((n, 2, 2, tokens, width), BF16),
            pltpu.VMEM((n, 2, tokens, width), F32),
            pltpu.VMEM((n, 2, tokens, width), BF16),
            pltpu.SemaphoreType.DMA((2, n, 2, 2)),
            pltpu.SemaphoreType.DMA((n, 2)),
            pltpu.SemaphoreType.DMA((n, 2)),
        ],
        input_output_aliases={} if first else {1 + 2 * n: 0, 2 + 2 * n: 1},
        compiler_params=PARAMS,
        cost_estimate=cost(n * tokens * width * 36),
        name="finish",
    )(*operands)


def write(heads, per_head, place, received, outs):
    n, _, tokens, width = received.shape

    def body(place_ref, src, *rest):
        targets, (low, wide, in_sem, out_sem) = rest[len(outs) : 2 * len(outs)], rest[2 * len(outs) :]
        other = 1 - lax.rem(place_ref[0], 2)
        loads = [pltpu.make_async_copy(src.at[x], low.at[x], in_sem.at[x]) for x in range(n)]
        for c in loads:
            c.start()
        waits = []
        for x in range(n):
            loads[x].wait()
            for t in range(2):
                wide[x, t] = low[x, t].astype(F32)
                head = other * MINE + heads[x]
                target = targets[0].at[:, 2 * head + t, 0, :] if per_head == 2 else targets[t].at[:, head, 0, :]
                waits.append(pltpu.make_async_copy(wide.at[x, t], target, out_sem.at[x, t]))
                waits[-1].start()
        for w in waits:
            w.wait()

    return pl.pallas_call(
        body,
        in_specs=[SCALAR, HBM] + [HBM] * len(outs),
        out_specs=[HBM] * len(outs),
        out_shape=[like(o.shape, F32) for o in outs],
        scratch_shapes=[
            pltpu.VMEM((n, 2, tokens, width), BF16),
            pltpu.VMEM((n, 2, tokens, width), F32),
            pltpu.SemaphoreType.DMA((n,)),
            pltpu.SemaphoreType.DMA((n, 2)),
        ],
        input_output_aliases={2 + i: i for i in range(len(outs))},
        compiler_params=PARAMS,
        cost_estimate=cost(n * tokens * width * 12),
        name="write",
    )(place, received, *outs)


def terms(query_tensor, key_tensor, value_tensor, output_gradient, logsumexp, row_inner_products):
    tokens, qheads, width = query_tensor.shape
    kheads = key_tensor.shape[1]
    place = lax.axis_index("seq").astype(jnp.int32).reshape(1)
    queries, gradients = (x.reshape(tokens, qheads, 1, width) for x in (query_tensor, output_gradient))
    keys, values = (x.reshape(tokens, kheads, 1, width) for x in (key_tensor, value_tensor))
    kv_mine, *parts, rows_mine = pack_kv(place, keys, values, logsumexp, row_inner_products)
    kv_give = parts.pop()
    groups = len(GROUPS)
    far = []
    for c in range(groups):
        far.append((rotated(parts[c], 2), crossed(parts[groups + c], 2)))
    kv_theirs = partner(kv_give)
    rows_theirs = partner(rows_mine)
    qg_give = pack_qg(True, place, queries, gradients)
    qg_theirs = partner(qg_give)
    qg_mine = pack_qg(False, place, queries, gradients)
    shared = (place, qg_mine, qg_theirs, rows_mine, rows_theirs, kv_mine, kv_theirs)
    query_grad = sent_dq = None
    own, back = [], []
    for c, size in enumerate(GROUPS):
        for slot in range(size):
            h = len(own)
            mine, theirs, query_grad, sent_dq = attend(h, slot, *shared, *far[c], query_grad, sent_dq)
            own.append(mine)
            back.append(rotated(theirs, -2))
    got_dq = partner(sent_dq)
    (query_grad,) = write(range(MINE), 2, place, got_dq, [query_grad])
    early = range(MINE - 1)
    key_grad, value_grad, send = finish(early, place, own[:-1], back[:-1], None, None)
    got = partner(send)
    key_grad, value_grad = write(early, 1, place, got, [key_grad, value_grad])
    last = [MINE - 1]
    key_grad, value_grad, send = finish(last, place, own[-1:], back[-1:], key_grad, value_grad)
    got = partner(send)
    key_grad, value_grad = write(last, 1, place, got, [key_grad, value_grad])
    return (
        query_grad.reshape(tokens, qheads, width),
        key_grad.reshape(tokens, kheads, width),
        value_grad.reshape(tokens, kheads, width),
    )


def solution(mesh):
    return jax.shard_map(
        terms,
        mesh=mesh,
        in_specs=(
            P("seq", "head", None),
            P("seq", "head", None),
            P("seq", "head", None),
            P("seq", "head", None),
            P("head", "seq"),
            P("head", "seq"),
        ),
        out_specs=(P("seq", "head", None), P("seq", "head", None), P("seq", "head", None)),
        check_vma=False,
    )
```

```python
import math

import jax
import jax.numpy as jnp
from jax import lax
from jax.experimental import pallas as pl
from jax.experimental.pallas import tpu as pltpu
from jax.sharding import PartitionSpec as P


QSCALE = 168
SCALE = QSCALE ** (-0.5)
LOG2E = math.log2(math.e)
VMEM = 24 * 1024 * 1024
GROUPS = (1, 1, 1, 1)
MINE = 4
F32, BF16 = jnp.float32, jnp.bfloat16
NT = (((1,), (1,)), ((), ()))
NN = (((1,), (0,)), ((), ()))
HBM = pl.BlockSpec(memory_space=pl.ANY)
GIVEN = pl.BlockSpec(memory_space=pltpu.HBM)
SCALAR = pl.BlockSpec(memory_space=pltpu.SMEM)
PARAMS = pltpu.CompilerParams(vmem_limit_bytes=VMEM)
ALONE = pltpu.CompilerParams(vmem_limit_bytes=64 * 1000 * 1024)


def dot(a, b, dims):
    return lax.dot_general(a, b, dims, preferred_element_type=F32)


def rotated(x, by):
    count = lax.axis_size("seq")
    return lax.ppermute(x, "seq", [(i, (i + by) % count) for i in range(count)])


def crossed(x, by):
    count = lax.axis_size("seq")
    return lax.ppermute(x, "seq", [(i, ((i + by) % count) ^ 1) for i in range(count)])


def partner(x):
    count = lax.axis_size("seq")
    return lax.ppermute(x, "seq", [(i, i ^ 1) for i in range(count)])


def cost(nbytes, flops=0, exps=0):
    return pl.CostEstimate(flops=flops, transcendentals=exps, bytes_accessed=nbytes)


def like(shape, dtype):
    return jax.ShapeDtypeStruct(shape, dtype)


def pack_kv(place, keys, values, lse, dots):
    tokens, heads, _, width = keys.shape

    def body(place_ref, k, v, lse_ref, dots_ref, *rest):
        keep, *parts, give, rows = rest[: 3 + 2 * len(GROUPS)]
        wide, narrow, rows_buf, in_sem, out_sem, part_sem, row_sem = rest[3 + 2 * len(GROUPS) :]
        spots = [(c, x) for c, n in enumerate(GROUPS) for x in range(n)]
        core = lax.rem(place_ref[0], 2)
        order = [(part, i) for part in range(2) for i in range(MINE)]

        def load(n, t):
            part, i = order[n]
            half = 1 - core if part == 0 else core
            return pltpu.make_async_copy((k, v)[t].at[:, half * MINE + i, 0, :], wide.at[n, t], in_sem.at[n, t])

        for n in range(len(order)):
            for t in range(2):
                load(n, t).start()
        row_loads = [pltpu.make_async_copy(x, rows_buf.at[t], row_sem.at[t]) for t, x in enumerate((lse_ref, dots_ref))]
        for c in row_loads:
            c.start()
        for c in row_loads:
            c.wait()
        waits = [pltpu.make_async_copy(rows_buf, rows, row_sem.at[2])]
        waits[0].start()
        for n, (part, i) in enumerate(order):
            for t in range(2):
                load(n, t).wait()
                narrow[n, t] = wide[n, t].astype(BF16)
            c, x = spots[i]
            target = parts[c if part else len(GROUPS) + c].at[x]
            waits.append(pltpu.make_async_copy(narrow.at[n], target, part_sem.at[n]))
            waits[-1].start()
            waits.append(pltpu.make_async_copy(narrow.at[n], (give, keep)[part].at[i], out_sem.at[n]))
            waits[-1].start()
        for w in waits:
            w.wait()

    return pl.pallas_call(
        body,
        in_specs=[SCALAR] + [GIVEN] * 4,
        out_specs=[HBM] * (3 + 2 * len(GROUPS)),
        out_shape=[
            like((MINE, 2, tokens, width), BF16),
            *[like((n, 2, tokens, width), BF16) for n in GROUPS] * 2,
            like((MINE, 2, tokens, width), BF16),
            like((2, *lse.shape), F32),
        ],
        scratch_shapes=[
            pltpu.VMEM((2 * MINE, 2, tokens, width), F32),
            pltpu.VMEM((2 * MINE, 2, tokens, width), BF16),
            pltpu.VMEM((2, *lse.shape), F32),
            pltpu.SemaphoreType.DMA((2 * MINE, 2)),
            pltpu.SemaphoreType.DMA((2 * MINE,)),
            pltpu.SemaphoreType.DMA((2 * MINE,)),
            pltpu.SemaphoreType.DMA((3,)),
        ],
        compiler_params=ALONE,
        cost_estimate=cost(tokens * heads * width * 12),
        name="pack_kv",
    )(place, keys, values, lse, dots)


def pack_qg(give, place, queries, gradients):
    tokens, _, _, width = queries.shape

    def body(place_ref, q, g, out, wide, narrow, in_sem, out_sem):
        core = lax.rem(place_ref[0], 2)
        half = 1 - core if give else core
        order = [(i, j, t) for i in range(MINE) for j in range(2) for t in range(2)]

        def load(i, j, t):
            return pltpu.make_async_copy(
                (q, g)[t].at[:, 2 * (half * MINE + i) + j, 0, :], wide.at[i, j, t], in_sem.at[i, j, t]
            )

        for o in order:
            load(*o).start()
        waits = []
        for i in range(MINE):
            for j in range(2):
                for t in range(2):
                    load(i, j, t).wait()
                    narrow[i, j, t] = wide[i, j, t].astype(BF16)
            waits.append(pltpu.make_async_copy(narrow.at[i], out.at[i], out_sem.at[i]))
            waits[-1].start()
        for w in waits:
            w.wait()

    shape = (MINE, 2, 2, tokens, width)
    return pl.pallas_call(
        body,
        in_specs=[SCALAR, GIVEN, GIVEN],
        out_specs=HBM,
        out_shape=like(shape, BF16),
        scratch_shapes=[
            pltpu.VMEM(shape, F32),
            pltpu.VMEM(shape, BF16),
            pltpu.SemaphoreType.DMA(shape[:3]),
            pltpu.SemaphoreType.DMA((MINE,)),
        ],
        compiler_params=ALONE,
        cost_estimate=cost(math.prod(shape) * 6),
        name="pack_qg",
    )(place, queries, gradients)


def attend(i, slot, place, qg_mine, qg_theirs, rows_mine, rows_theirs, kv_mine, kv_theirs, far_mine, far_theirs, query_grad, sent_dq):
    tokens, width = kv_mine.shape[2:]
    half = tokens // 2
    first = query_grad is None

    def body(place_ref, qm, qt, rm, rt, km, kt_, fm, ft, *rest):
        own, far, dq_out, dq_sent = rest[-17:-13]
        qg, rows_buf, keys, buf, low, sums, far_buf, in_sem, q_sem, sem, low_sem, own_sem, far_sem = rest[-13:]
        pos = place_ref[0]
        core = lax.rem(pos, 2)
        gate = jnp.where(pos >= 2, 0.0, 1e30).astype(F32)
        head = core * MINE + i
        sides = ((core, 0), (1 - core, 1))
        copy = pltpu.make_async_copy
        loads = [copy((rm, rt)[x], rows_buf.at[n], in_sem.at[x]) for n, x in sides]
        loads += [copy((km, kt_)[x].at[i], keys.at[0, n], in_sem.at[2 + x]) for n, x in sides]
        loads += [copy((fm, ft)[x].at[slot], keys.at[1, n], in_sem.at[4 + x]) for n, x in sides]

        def q_loads(j):
            return [
                copy(qm.at[i, j], qg.at[j, core], q_sem.at[j, 0]),
                copy(qt.at[i, j], qg.at[j, 1 - core], q_sem.at[j, 1]),
            ]

        def dq_copies(j):
            return [
                copy(buf.at[core, j], dq_out.at[:, 2 * head + j, 0, :], sem.at[j]),
                copy(low.at[1 - core, j], dq_sent.at[i, j], low_sem.at[j]),
            ]

        for c in loads + q_loads(0) + q_loads(1):
            c.start()
        for c in loads:
            c.wait()
        rows = lax.broadcasted_iota(jnp.int32, (half, half), 0)
        cols = lax.broadcasted_iota(jnp.int32, (half, half), 1)
        later = rows > cols
        cut = [(a // 2, slice((a % 2) * half, (a % 2 + 1) * half)) for a in range(4)]
        tiles = [(e, a) for e in range(2) for a in range(4)]

        def one_head(j, _):
            kb = {(e, a): keys[e, cut[a][0], 0, cut[a][1], :] for e, a in tiles}
            vb = {(e, a): keys[e, cut[a][0], 1, cut[a][1], :] for e, a in tiles}
            kt = {x: kb[x].T for x in tiles}
            dk, dv = {x: [] for x in tiles}, {x: [] for x in tiles}
            for c in q_loads(j):
                c.wait()
            row = pl.ds(2 * head + j, 1)
            for b, (n, sl) in enumerate(cut):
                q, g = qg[j, n, 0, sl, :], qg[j, n, 1, sl, :]
                l = rows_buf[n, 0, row, sl] * LOG2E
                d = rows_buf[n, 1, row, sl]
                dqt = []
                for e, a in [(0, a) for a in range(b + 1)] + [(1, a) for a in range(b, 4)]:
                    p = jnp.exp2(dot(kb[e, a], q, NT) * (SCALE * LOG2E) - (l + gate if e else l))
                    if a == b:
                        p = jnp.where(later, p, 0.0) if e else jnp.where(later, 0.0, p)
                    ds = (p * (dot(vb[e, a], g, NT) - d)).astype(BF16)
                    dv[e, a].append((p.astype(BF16), g))
                    dk[e, a].append((ds, q))
                    dqt.append((kt[e, a], ds))
                x = (sum(dot(x, y, NN) for x, y in dqt) * SCALE).T
                buf[n, j, sl, :] = x
                low[n, j, sl, :] = x.astype(BF16)
            for c in dq_copies(j):
                c.start()
            for e, a in tiles:
                where = slice(a * half, (a + 1) * half)
                for t in range(2):
                    x = sum(dot(x, y, NN) for x, y in (dv if t else dk)[e, a])
                    x = (x if t else x * SCALE) + jnp.where(j == 0, 0.0, sums[e, t, where, :])
                    sums[e, t, where, :] = x
                    if e:
                        far_buf[t, where, :] = x.astype(BF16)
            return 0

        lax.fori_loop(0, 2, one_head, 0)
        out_copies = [copy(sums.at[0], own, own_sem), copy(far_buf, far, far_sem)]
        for c in out_copies:
            c.start()
        for c in dq_copies(0) + dq_copies(1) + out_copies:
            c.wait()

    operands = [place, qg_mine, qg_theirs, rows_mine, rows_theirs, kv_mine, kv_theirs, far_mine, far_theirs]
    in_specs = [SCALAR] + [HBM] * 8
    if not first:
        operands += [query_grad, sent_dq]
        in_specs += [HBM, HBM]
    return pl.pallas_call(
        body,
        in_specs=in_specs,
        out_specs=[HBM] * 4,
        out_shape=[
            like((2, 2 * tokens, width), F32),
            like((2, 2 * tokens, width), BF16),
            like((tokens, 4 * MINE, 1, width), F32),
            like((MINE, 2, tokens, width), BF16),
        ],
        scratch_shapes=[
            pltpu.VMEM((2, 2, 2, tokens, width), BF16),
            pltpu.VMEM((2, *rows_mine.shape), F32),
            pltpu.VMEM((2, 2, 2, tokens, width), BF16),
            pltpu.VMEM((2, 2, tokens, width), F32),
            pltpu.VMEM((2, 2, tokens, width), BF16),
            pltpu.VMEM((2, 2, 2 * tokens, width), F32),
            pltpu.VMEM((2, 2 * tokens, width), BF16),
            pltpu.SemaphoreType.DMA((6,)),
            pltpu.SemaphoreType.DMA((2, 2)),
            pltpu.SemaphoreType.DMA((2,)),
            pltpu.SemaphoreType.DMA((2,)),
            pltpu.SemaphoreType.DMA,
            pltpu.SemaphoreType.DMA,
        ],
        input_output_aliases={} if first else {9: 2, 10: 3},
        compiler_params=PARAMS,
        cost_estimate=cost(tokens * width * 40, 2 * 20 * 5 * 2 * half**2 * width, 2 * 20 * half**2),
        name="attend",
    )(*operands)


def finish(heads, place, owns, backs, key_grad, value_grad):
    tokens, width = owns[0].shape[1] // 2, owns[0].shape[2]
    n = len(heads)
    first = key_grad is None

    def body(place_ref, *rest):
        own_refs, back_refs, (dk, dv, send) = rest[:n], rest[n : 2 * n], rest[-10:-7]
        own_buf, back_buf, out_buf, low, in_sem, out_sem, low_sem = rest[-7:]
        core = lax.rem(place_ref[0], 2)
        order = [(x, side, t) for x in range(n) for side in range(2) for t in range(2)]

        def loads(x, side, t):
            where = pl.ds(pl.multiple_of((core if side else 1 - core) * tokens, tokens), tokens)
            return [
                pltpu.make_async_copy(own_refs[x].at[t, where, :], own_buf.at[x, side, t], in_sem.at[0, x, side, t]),
                pltpu.make_async_copy(back_refs[x].at[t, where, :], back_buf.at[x, side, t], in_sem.at[1, x, side, t]),
            ]

        for o in order:
            for c in loads(*o):
                c.start()
        waits = []
        for x, side, t in order:
            for c in loads(x, side, t):
                c.wait()
            total = own_buf[x, side, t] + back_buf[x, side, t].astype(F32)
            if side:
                out_buf[x, t] = total
                target = (dk, dv)[t].at[:, core * MINE + heads[x], 0, :]
                waits.append(pltpu.make_async_copy(out_buf.at[x, t], target, out_sem.at[x, t]))
            else:
                low[x, t] = total.astype(BF16)
                waits.append(pltpu.make_async_copy(low.at[x, t], send.at[x, t], low_sem.at[x, t]))
            waits[-1].start()
        for w in waits:
            w.wait()

    operands = [place, *owns, *backs]
    in_specs = [SCALAR] + [HBM] * (2 * n)
    if not first:
        operands += [key_grad, value_grad]
        in_specs += [HBM, HBM]
    return pl.pallas_call(
        body,
        in_specs=in_specs,
        out_specs=[HBM] * 3,
        out_shape=[like((tokens, 2 * MINE, 1, width), F32)] * 2 + [like((n, 2, tokens, width), BF16)],
        scratch_shapes=[
            pltpu.VMEM((n, 2, 2, tokens, width), F32),
            pltpu.VMEM((n, 2, 2, tokens, width), BF16),
            pltpu.VMEM((n, 2, tokens, width), F32),
            pltpu.VMEM((n, 2, tokens, width), BF16),
            pltpu.SemaphoreType.DMA((2, n, 2, 2)),
            pltpu.SemaphoreType.DMA((n, 2)),
            pltpu.SemaphoreType.DMA((n, 2)),
        ],
        input_output_aliases={} if first else {1 + 2 * n: 0, 2 + 2 * n: 1},
        compiler_params=PARAMS,
        cost_estimate=cost(n * tokens * width * 36),
        name="finish",
    )(*operands)


def write(heads, per_head, place, received, outs):
    n, _, tokens, width = received.shape

    def body(place_ref, src, *rest):
        targets, (low, wide, in_sem, out_sem) = rest[len(outs) : 2 * len(outs)], rest[2 * len(outs) :]
        other = 1 - lax.rem(place_ref[0], 2)
        loads = [pltpu.make_async_copy(src.at[x], low.at[x], in_sem.at[x]) for x in range(n)]
        for c in loads:
            c.start()
        waits = []
        for x in range(n):
            loads[x].wait()
            for t in range(2):
                wide[x, t] = low[x, t].astype(F32)
                head = other * MINE + heads[x]
                target = targets[0].at[:, 2 * head + t, 0, :] if per_head == 2 else targets[t].at[:, head, 0, :]
                waits.append(pltpu.make_async_copy(wide.at[x, t], target, out_sem.at[x, t]))
                waits[-1].start()
        for w in waits:
            w.wait()

    return pl.pallas_call(
        body,
        in_specs=[SCALAR, HBM] + [HBM] * len(outs),
        out_specs=[HBM] * len(outs),
        out_shape=[like(o.shape, F32) for o in outs],
        scratch_shapes=[
            pltpu.VMEM((n, 2, tokens, width), BF16),
            pltpu.VMEM((n, 2, tokens, width), F32),
            pltpu.SemaphoreType.DMA((n,)),
            pltpu.SemaphoreType.DMA((n, 2)),
        ],
        input_output_aliases={2 + i: i for i in range(len(outs))},
        compiler_params=PARAMS,
        cost_estimate=cost(n * tokens * width * 12),
        name="write",
    )(place, received, *outs)


def terms(query_tensor, key_tensor, value_tensor, output_gradient, logsumexp, row_inner_products):
    tokens, qheads, width = query_tensor.shape
    kheads = key_tensor.shape[1]
    place = lax.axis_index("seq").astype(jnp.int32).reshape(1)
    queries, gradients = (x.reshape(tokens, qheads, 1, width) for x in (query_tensor, output_gradient))
    keys, values = (x.reshape(tokens, kheads, 1, width) for x in (key_tensor, value_tensor))
    kv_mine, *parts, rows_mine = pack_kv(place, keys, values, logsumexp, row_inner_products)
    kv_give = parts.pop()
    groups = len(GROUPS)
    far = []
    for c in range(groups):
        far.append((rotated(parts[c], 2), crossed(parts[groups + c], 2)))
    kv_theirs = partner(kv_give)
    rows_theirs = partner(rows_mine)
    qg_give = pack_qg(True, place, queries, gradients)
    qg_theirs = partner(qg_give)
    qg_mine = pack_qg(False, place, queries, gradients)
    shared = (place, qg_mine, qg_theirs, rows_mine, rows_theirs, kv_mine, kv_theirs)
    query_grad = sent_dq = None
    own, back = [], []
    for c, size in enumerate(GROUPS):
        for slot in range(size):
            h = len(own)
            mine, theirs, query_grad, sent_dq = attend(h, slot, *shared, *far[c], query_grad, sent_dq)
            own.append(mine)
            back.append(rotated(theirs, -2))
    got_dq = partner(sent_dq)
    (query_grad,) = write(range(MINE), 2, place, got_dq, [query_grad])
    early = range(MINE - 1)
    key_grad, value_grad, send = finish(early, place, own[:-1], back[:-1], None, None)
    got = partner(send)
    key_grad, value_grad = write(early, 1, place, got, [key_grad, value_grad])
    last = [MINE - 1]
    key_grad, value_grad, send = finish(last, place, own[-1:], back[-1:], key_grad, value_grad)
    got = partner(send)
    key_grad, value_grad = write(last, 1, place, got, [key_grad, value_grad])
    return (
        query_grad.reshape(tokens, qheads, width),
        key_grad.reshape(tokens, kheads, width),
        value_grad.reshape(tokens, kheads, width),
    )


def solution(mesh):
    return jax.shard_map(
        terms,
        mesh=mesh,
        in_specs=(
            P("seq", "head", None),
            P("seq", "head", None),
            P("seq", "head", None),
            P("seq", "head", None),
            P("head", "seq"),
            P("head", "seq"),
        ),
        out_specs=(P("seq", "head", None), P("seq", "head", None), P("seq", "head", None)),
        check_vma=False,
    )
```

```python
import math

import jax
import jax.numpy as jnp
from jax import lax
from jax.experimental import pallas as pl
from jax.experimental.pallas import tpu as pltpu
from jax.sharding import PartitionSpec as P


QSCALE = 168
SCALE = QSCALE ** (-0.5)
LOG2E = math.log2(math.e)
VMEM = 24 * 1024 * 1024
GROUPS = (1, 1, 1, 1)
MINE = 4
F32, BF16 = jnp.float32, jnp.bfloat16
NT = (((1,), (1,)), ((), ()))
NN = (((1,), (0,)), ((), ()))
HBM = pl.BlockSpec(memory_space=pl.ANY)
GIVEN = pl.BlockSpec(memory_space=pltpu.HBM)
SCALAR = pl.BlockSpec(memory_space=pltpu.SMEM)
PARAMS = pltpu.CompilerParams(vmem_limit_bytes=VMEM)
ALONE = pltpu.CompilerParams(vmem_limit_bytes=64 * 1000 * 1024)


def dot(a, b, dims):
    return lax.dot_general(a, b, dims, preferred_element_type=F32)


def rotated(x, by):
    count = lax.axis_size("seq")
    return lax.ppermute(x, "seq", [(i, (i + by) % count) for i in range(count)])


def crossed(x, by):
    count = lax.axis_size("seq")
    return lax.ppermute(x, "seq", [(i, ((i + by) % count) ^ 1) for i in range(count)])


def partner(x):
    count = lax.axis_size("seq")
    return lax.ppermute(x, "seq", [(i, i ^ 1) for i in range(count)])


def cost(nbytes, flops=0, exps=0):
    return pl.CostEstimate(flops=flops, transcendentals=exps, bytes_accessed=nbytes)


def like(shape, dtype):
    return jax.ShapeDtypeStruct(shape, dtype)


def pack_kv(place, keys, values, lse, dots):
    tokens, heads, _, width = keys.shape

    def body(place_ref, k, v, lse_ref, dots_ref, *rest):
        keep, *parts, give, rows = rest[: 3 + 2 * len(GROUPS)]
        wide, narrow, rows_buf, in_sem, out_sem, part_sem, row_sem = rest[3 + 2 * len(GROUPS) :]
        spots = [(c, x) for c, n in enumerate(GROUPS) for x in range(n)]
        core = lax.rem(place_ref[0], 2)
        order = [(part, i) for part in range(2) for i in range(MINE)]

        def load(n, t):
            part, i = order[n]
            half = 1 - core if part == 0 else core
            return pltpu.make_async_copy((k, v)[t].at[:, half * MINE + i, 0, :], wide.at[n, t], in_sem.at[n, t])

        for n in range(len(order)):
            for t in range(2):
                load(n, t).start()
        row_loads = [pltpu.make_async_copy(x, rows_buf.at[t], row_sem.at[t]) for t, x in enumerate((lse_ref, dots_ref))]
        for c in row_loads:
            c.start()
        for c in row_loads:
            c.wait()
        waits = [pltpu.make_async_copy(rows_buf, rows, row_sem.at[2])]
        waits[0].start()
        for n, (part, i) in enumerate(order):
            for t in range(2):
                load(n, t).wait()
                narrow[n, t] = wide[n, t].astype(BF16)
            c, x = spots[i]
            target = parts[c if part else len(GROUPS) + c].at[x]
            waits.append(pltpu.make_async_copy(narrow.at[n], target, part_sem.at[n]))
            waits[-1].start()
            waits.append(pltpu.make_async_copy(narrow.at[n], (give, keep)[part].at[i], out_sem.at[n]))
            waits[-1].start()
        for w in waits:
            w.wait()

    return pl.pallas_call(
        body,
        in_specs=[SCALAR] + [GIVEN] * 4,
        out_specs=[HBM] * (3 + 2 * len(GROUPS)),
        out_shape=[
            like((MINE, 2, tokens, width), BF16),
            *[like((n, 2, tokens, width), BF16) for n in GROUPS] * 2,
            like((MINE, 2, tokens, width), BF16),
            like((2, *lse.shape), F32),
        ],
        scratch_shapes=[
            pltpu.VMEM((2 * MINE, 2, tokens, width), F32),
            pltpu.VMEM((2 * MINE, 2, tokens, width), BF16),
            pltpu.VMEM((2, *lse.shape), F32),
            pltpu.SemaphoreType.DMA((2 * MINE, 2)),
            pltpu.SemaphoreType.DMA((2 * MINE,)),
            pltpu.SemaphoreType.DMA((2 * MINE,)),
            pltpu.SemaphoreType.DMA((3,)),
        ],
        compiler_params=ALONE,
        cost_estimate=cost(tokens * heads * width * 12),
        name="pack_kv",
    )(place, keys, values, lse, dots)


def pack_qg(give, place, queries, gradients):
    tokens, _, _, width = queries.shape

    def body(place_ref, q, g, out, wide, narrow, in_sem, out_sem):
        core = lax.rem(place_ref[0], 2)
        half = 1 - core if give else core
        order = [(i, j, t) for i in range(MINE) for j in range(2) for t in range(2)]

        def load(i, j, t):
            return pltpu.make_async_copy(
                (q, g)[t].at[:, 2 * (half * MINE + i) + j, 0, :], wide.at[i, j, t], in_sem.at[i, j, t]
            )

        for o in order:
            load(*o).start()
        waits = []
        for i in range(MINE):
            for j in range(2):
                for t in range(2):
                    load(i, j, t).wait()
                    narrow[i, j, t] = wide[i, j, t].astype(BF16)
            waits.append(pltpu.make_async_copy(narrow.at[i], out.at[i], out_sem.at[i]))
            waits[-1].start()
        for w in waits:
            w.wait()

    shape = (MINE, 2, 2, tokens, width)
    return pl.pallas_call(
        body,
        in_specs=[SCALAR, GIVEN, GIVEN],
        out_specs=HBM,
        out_shape=like(shape, BF16),
        scratch_shapes=[
            pltpu.VMEM(shape, F32),
            pltpu.VMEM(shape, BF16),
            pltpu.SemaphoreType.DMA(shape[:3]),
            pltpu.SemaphoreType.DMA((MINE,)),
        ],
        compiler_params=ALONE,
        cost_estimate=cost(math.prod(shape) * 6),
        name="pack_qg",
    )(place, queries, gradients)


def attend(i, slot, place, qg_mine, qg_theirs, rows_mine, rows_theirs, kv_mine, kv_theirs, far_mine, far_theirs, query_grad, sent_dq, split):
    tokens, width = kv_mine.shape[2:]
    half = tokens // 2
    first = query_grad is None

    def body(place_ref, qm, qt, rm, rt, km, kt_, fm, ft, *rest):
        own, *others, dq_out, dq_sent = rest[-15 - (6 if split else 4) : -15]
        qg, rows_buf, keys, buf, low, sums, far_buf, own_low, in_sem, q_sem, sem, low_sem, own_sem, far_sem, give_sem = rest[-15:]
        pos = place_ref[0]
        core = lax.rem(pos, 2)
        gate = jnp.where(pos >= 2, 0.0, 1e30).astype(F32)
        head = core * MINE + i
        sides = ((core, 0), (1 - core, 1))
        copy = pltpu.make_async_copy
        loads = [copy((rm, rt)[x], rows_buf.at[n], in_sem.at[x]) for n, x in sides]
        loads += [copy((km, kt_)[x].at[i], keys.at[0, n], in_sem.at[2 + x]) for n, x in sides]
        loads += [copy((fm, ft)[x].at[slot], keys.at[1, n], in_sem.at[4 + x]) for n, x in sides]

        def q_loads(j):
            return [
                copy(qm.at[i, j], qg.at[j, core], q_sem.at[j, 0]),
                copy(qt.at[i, j], qg.at[j, 1 - core], q_sem.at[j, 1]),
            ]

        def dq_copies(j):
            return [
                copy(buf.at[core, j], dq_out.at[:, 2 * head + j, 0, :], sem.at[j]),
                copy(low.at[1 - core, j], dq_sent.at[i, j], low_sem.at[j]),
            ]

        for c in loads + q_loads(0) + q_loads(1):
            c.start()
        for c in loads:
            c.wait()
        rows = lax.broadcasted_iota(jnp.int32, (half, half), 0)
        cols = lax.broadcasted_iota(jnp.int32, (half, half), 1)
        later = rows > cols
        cut = [(a // 2, slice((a % 2) * half, (a % 2 + 1) * half)) for a in range(4)]
        tiles = [(e, a) for e in range(2) for a in range(4)]

        def one_head(j, _):
            kb = {(e, a): keys[e, cut[a][0], 0, cut[a][1], :] for e, a in tiles}
            vb = {(e, a): keys[e, cut[a][0], 1, cut[a][1], :] for e, a in tiles}
            kt = {x: kb[x].T for x in tiles}
            dk, dv = {x: [] for x in tiles}, {x: [] for x in tiles}
            for c in q_loads(j):
                c.wait()
            row = pl.ds(2 * head + j, 1)
            for b, (n, sl) in enumerate(cut):
                q, g = qg[j, n, 0, sl, :], qg[j, n, 1, sl, :]
                l = rows_buf[n, 0, row, sl] * LOG2E
                d = rows_buf[n, 1, row, sl]
                dqt = []
                for e, a in [(0, a) for a in range(b + 1)] + [(1, a) for a in range(b, 4)]:
                    p = jnp.exp2(dot(kb[e, a], q, NT) * (SCALE * LOG2E) - (l + gate if e else l))
                    if a == b:
                        p = jnp.where(later, p, 0.0) if e else jnp.where(later, 0.0, p)
                    ds = (p * (dot(vb[e, a], g, NT) - d)).astype(BF16)
                    dv[e, a].append((p.astype(BF16), g))
                    dk[e, a].append((ds, q))
                    dqt.append((kt[e, a], ds))
                x = (sum(dot(x, y, NN) for x, y in dqt) * SCALE).T
                buf[n, j, sl, :] = x
                low[n, j, sl, :] = x.astype(BF16)
            for c in dq_copies(j):
                c.start()
            for e, a in tiles:
                where = slice(a * half, (a + 1) * half)
                for t in range(2):
                    x = sum(dot(x, y, NN) for x, y in (dv if t else dk)[e, a])
                    x = (x if t else x * SCALE) + jnp.where(j == 0, 0.0, sums[e, t, where, :])
                    sums[e, t, where, :] = x
                    if e:
                        far_buf[t, where, :] = x.astype(BF16)
                    elif split:
                        own_low[t, where, :] = x.astype(BF16)
            return 0

        lax.fori_loop(0, 2, one_head, 0)
        out_copies = [copy(sums.at[0], own, own_sem)]
        if split:
            keep, give = (pl.ds(pl.multiple_of(x * tokens, tokens), tokens) for x in (core, 1 - core))
            out_copies.append(copy(far_buf.at[:, keep, :], others[0], far_sem))
            out_copies.append(copy(far_buf.at[:, give, :], others[1], give_sem.at[0]))
            out_copies.append(copy(own_low.at[:, give, :], others[2], give_sem.at[1]))
        else:
            out_copies.append(copy(far_buf, others[0], far_sem))
        for c in out_copies:
            c.start()
        for c in dq_copies(0) + dq_copies(1) + out_copies:
            c.wait()

    operands = [place, qg_mine, qg_theirs, rows_mine, rows_theirs, kv_mine, kv_theirs, far_mine, far_theirs]
    in_specs = [SCALAR] + [HBM] * 8
    if not first:
        operands += [query_grad, sent_dq]
        in_specs += [HBM, HBM]
    return pl.pallas_call(
        body,
        in_specs=in_specs,
        out_specs=[HBM] * (6 if split else 4),
        out_shape=[
            like((2, 2 * tokens, width), F32),
            *([like((2, tokens, width), BF16)] * 3 if split else [like((2, 2 * tokens, width), BF16)]),
            like((tokens, 4 * MINE, 1, width), F32),
            like((MINE, 2, tokens, width), BF16),
        ],
        scratch_shapes=[
            pltpu.VMEM((2, 2, 2, tokens, width), BF16),
            pltpu.VMEM((2, *rows_mine.shape), F32),
            pltpu.VMEM((2, 2, 2, tokens, width), BF16),
            pltpu.VMEM((2, 2, tokens, width), F32),
            pltpu.VMEM((2, 2, tokens, width), BF16),
            pltpu.VMEM((2, 2, 2 * tokens, width), F32),
            pltpu.VMEM((2, 2 * tokens, width), BF16),
            pltpu.VMEM((2, 2 * tokens, width), BF16),
            pltpu.SemaphoreType.DMA((6,)),
            pltpu.SemaphoreType.DMA((2, 2)),
            pltpu.SemaphoreType.DMA((2,)),
            pltpu.SemaphoreType.DMA((2,)),
            pltpu.SemaphoreType.DMA,
            pltpu.SemaphoreType.DMA,
            pltpu.SemaphoreType.DMA((2,)),
        ],
        input_output_aliases={} if first else {9: 4, 10: 5} if split else {9: 2, 10: 3},
        compiler_params=PARAMS,
        cost_estimate=cost(tokens * width * 40, 2 * 20 * 5 * 2 * half**2 * width, 2 * 20 * half**2),
        name="attend",
    )(*operands)


def finish(heads, place, owns, backs, key_grad, value_grad):
    tokens, width = owns[0].shape[1] // 2, owns[0].shape[2]
    n = len(heads)
    first = key_grad is None

    def body(place_ref, *rest):
        own_refs, back_refs, (dk, dv, send) = rest[:n], rest[n : 2 * n], rest[-10:-7]
        own_buf, back_buf, out_buf, low, in_sem, out_sem, low_sem = rest[-7:]
        core = lax.rem(place_ref[0], 2)
        order = [(x, side, t) for x in range(n) for side in range(2) for t in range(2)]

        def loads(x, side, t):
            where = pl.ds(pl.multiple_of((core if side else 1 - core) * tokens, tokens), tokens)
            return [
                pltpu.make_async_copy(own_refs[x].at[t, where, :], own_buf.at[x, side, t], in_sem.at[0, x, side, t]),
                pltpu.make_async_copy(back_refs[x].at[t, where, :], back_buf.at[x, side, t], in_sem.at[1, x, side, t]),
            ]

        for o in order:
            for c in loads(*o):
                c.start()
        waits = []
        for x, side, t in order:
            for c in loads(x, side, t):
                c.wait()
            total = own_buf[x, side, t] + back_buf[x, side, t].astype(F32)
            if side:
                out_buf[x, t] = total
                target = (dk, dv)[t].at[:, core * MINE + heads[x], 0, :]
                waits.append(pltpu.make_async_copy(out_buf.at[x, t], target, out_sem.at[x, t]))
            else:
                low[x, t] = total.astype(BF16)
                waits.append(pltpu.make_async_copy(low.at[x, t], send.at[x, t], low_sem.at[x, t]))
            waits[-1].start()
        for w in waits:
            w.wait()

    operands = [place, *owns, *backs]
    in_specs = [SCALAR] + [HBM] * (2 * n)
    if not first:
        operands += [key_grad, value_grad]
        in_specs += [HBM, HBM]
    return pl.pallas_call(
        body,
        in_specs=in_specs,
        out_specs=[HBM] * 3,
        out_shape=[like((tokens, 2 * MINE, 1, width), F32)] * 2 + [like((n, 2, tokens, width), BF16)],
        scratch_shapes=[
            pltpu.VMEM((n, 2, 2, tokens, width), F32),
            pltpu.VMEM((n, 2, 2, tokens, width), BF16),
            pltpu.VMEM((n, 2, tokens, width), F32),
            pltpu.VMEM((n, 2, tokens, width), BF16),
            pltpu.SemaphoreType.DMA((2, n, 2, 2)),
            pltpu.SemaphoreType.DMA((n, 2)),
            pltpu.SemaphoreType.DMA((n, 2)),
        ],
        input_output_aliases={} if first else {1 + 2 * n: 0, 2 + 2 * n: 1},
        compiler_params=PARAMS,
        cost_estimate=cost(n * tokens * width * 36),
        name="finish",
    )(*operands)


def write(heads, per_head, place, received, outs):
    n, _, tokens, width = received.shape

    def body(place_ref, src, *rest):
        targets, (low, wide, in_sem, out_sem) = rest[len(outs) : 2 * len(outs)], rest[2 * len(outs) :]
        other = 1 - lax.rem(place_ref[0], 2)
        loads = [pltpu.make_async_copy(src.at[x], low.at[x], in_sem.at[x]) for x in range(n)]
        for c in loads:
            c.start()
        waits = []
        for x in range(n):
            loads[x].wait()
            for t in range(2):
                wide[x, t] = low[x, t].astype(F32)
                head = other * MINE + heads[x]
                target = targets[0].at[:, 2 * head + t, 0, :] if per_head == 2 else targets[t].at[:, head, 0, :]
                waits.append(pltpu.make_async_copy(wide.at[x, t], target, out_sem.at[x, t]))
                waits[-1].start()
        for w in waits:
            w.wait()

    return pl.pallas_call(
        body,
        in_specs=[SCALAR, HBM] + [HBM] * len(outs),
        out_specs=[HBM] * len(outs),
        out_shape=[like(o.shape, F32) for o in outs],
        scratch_shapes=[
            pltpu.VMEM((n, 2, tokens, width), BF16),
            pltpu.VMEM((n, 2, tokens, width), F32),
            pltpu.SemaphoreType.DMA((n,)),
            pltpu.SemaphoreType.DMA((n, 2)),
        ],
        input_output_aliases={2 + i: i for i in range(len(outs))},
        compiler_params=PARAMS,
        cost_estimate=cost(n * tokens * width * 12),
        name="write",
    )(place, received, *outs)


def finish_last(head, place, own, got_own, back_keep, back_cross, key_grad, value_grad):
    tokens, width = back_keep.shape[1:]

    def body(place_ref, own_ref, got_ref, keep_ref, cross_ref, *rest):
        (dk, dv), (wide, low, out_buf, wide_sem, low_sem, out_sem) = rest[2:4], rest[4:]
        core = lax.rem(place_ref[0], 2)
        copy = pltpu.make_async_copy
        mine = pl.ds(pl.multiple_of(core * tokens, tokens), tokens)
        order = [(side, t) for t in range(2) for side in range(2)]

        def loads(side, t):
            if side:
                return [
                    copy(got_ref.at[t], low.at[1, t], low_sem.at[1, t]),
                    copy(cross_ref.at[t], low.at[2, t], low_sem.at[2, t]),
                ]
            return [
                copy(own_ref.at[t, mine, :], wide.at[t], wide_sem.at[t]),
                copy(keep_ref.at[t], low.at[0, t], low_sem.at[0, t]),
            ]

        for o in order:
            for c in loads(*o):
                c.start()
        waits = []
        for side, t in order:
            for c in loads(side, t):
                c.wait()
            if side:
                out_buf[1, t] = low[1, t].astype(F32) + low[2, t].astype(F32)
            else:
                out_buf[0, t] = wide[t] + low[0, t].astype(F32)
            target = (dk, dv)[t].at[:, (1 - core if side else core) * MINE + head, 0, :]
            waits.append(copy(out_buf.at[side, t], target, out_sem.at[side, t]))
            waits[-1].start()
        for w in waits:
            w.wait()

    return pl.pallas_call(
        body,
        in_specs=[SCALAR] + [HBM] * 6,
        out_specs=[HBM] * 2,
        out_shape=[like(key_grad.shape, F32)] * 2,
        scratch_shapes=[
            pltpu.VMEM((2, tokens, width), F32),
            pltpu.VMEM((3, 2, tokens, width), BF16),
            pltpu.VMEM((2, 2, tokens, width), F32),
            pltpu.SemaphoreType.DMA((2,)),
            pltpu.SemaphoreType.DMA((3, 2)),
            pltpu.SemaphoreType.DMA((2, 2)),
        ],
        input_output_aliases={5: 0, 6: 1},
        compiler_params=PARAMS,
        cost_estimate=cost(tokens * width * 36),
        name="finish_last",
    )(place, own, got_own, back_keep, back_cross, key_grad, value_grad)


def terms(query_tensor, key_tensor, value_tensor, output_gradient, logsumexp, row_inner_products):
    tokens, qheads, width = query_tensor.shape
    kheads = key_tensor.shape[1]
    place = lax.axis_index("seq").astype(jnp.int32).reshape(1)
    queries, gradients = (x.reshape(tokens, qheads, 1, width) for x in (query_tensor, output_gradient))
    keys, values = (x.reshape(tokens, kheads, 1, width) for x in (key_tensor, value_tensor))
    kv_mine, *parts, rows_mine = pack_kv(place, keys, values, logsumexp, row_inner_products)
    kv_give = parts.pop()
    groups = len(GROUPS)
    far = []
    for c in range(groups):
        far.append((rotated(parts[c], 2), crossed(parts[groups + c], 2)))
    kv_theirs = partner(kv_give)
    rows_theirs = partner(rows_mine)
    qg_give = pack_qg(True, place, queries, gradients)
    qg_theirs = partner(qg_give)
    qg_mine = pack_qg(False, place, queries, gradients)
    shared = (place, qg_mine, qg_theirs, rows_mine, rows_theirs, kv_mine, kv_theirs)
    query_grad = sent_dq = None
    own, back = [], []
    for c, size in enumerate(GROUPS):
        for slot in range(size):
            h = len(own)
            mine, *theirs, query_grad, sent_dq = attend(h, slot, *shared, *far[c], query_grad, sent_dq, h == MINE - 1)
            own.append(mine)
            back.append(rotated(theirs[0], -2))
    back_cross = crossed(theirs[1], -2)
    got_dq = partner(sent_dq)
    (query_grad,) = write(range(MINE), 2, place, got_dq, [query_grad])
    got_own = partner(theirs[2])
    early = range(MINE - 1)
    key_grad, value_grad, send = finish(early, place, own[:-1], back[:-1], None, None)
    got = partner(send)
    key_grad, value_grad = write(early, 1, place, got, [key_grad, value_grad])
    key_grad, value_grad = finish_last(MINE - 1, place, own[-1], got_own, back[-1], back_cross, key_grad, value_grad)
    return (
        query_grad.reshape(tokens, qheads, width),
        key_grad.reshape(tokens, kheads, width),
        value_grad.reshape(tokens, kheads, width),
    )


def solution(mesh):
    return jax.shard_map(
        terms,
        mesh=mesh,
        in_specs=(
            P("seq", "head", None),
            P("seq", "head", None),
            P("seq", "head", None),
            P("seq", "head", None),
            P("head", "seq"),
            P("head", "seq"),
        ),
        out_specs=(P("seq", "head", None), P("seq", "head", None), P("seq", "head", None)),
        check_vma=False,
    )
```
